512 devices in a mesh: tm: 16 (over y, core), sta: 32 (over z, x).
Axes of the slice: x: 4, y: 8, z: 8, core: 2. Of those that a mesh axis runs over, the one named last changes fastest.
Arguments:
- spectra: bfloat16 [16, 2048, 2048], P('tm', 'sta'), may hold values from -5 to 5
- pair_list: int32 [16, 32, 256], P('tm', 'sta'), may hold values from 0 to 511, as said below
- pair_stations: int32 [2, 16384], P(None, 'sta'), may hold values from 0 to 2047
- owner_code: int32 [16384], P('sta'), may hold values from 0 to 1023, as said below
Outputs:
- stack: float32 [32768, 1024], P(('tm', 'sta'))
The draws below stay inside these ranges and needn't reach their ends.
Inputs may be any that keep to these rules, and one draw needn't show every extreme that they name: `pair_list`: within each (g, s) the entries are distinct catalogue numbers below 512. `owner_code`: within each catalogue of 512 pairs the codes are distinct; each owner (code // 64) holds at most 64 pairs of a catalogue, and in every catalogue one owner holds exactly 64.
All inputs are finite; a program needn't handle non-finite values.
Results may differ from the reference program's by a relative error of at most 0.0003.
Values may be sent and summed in bfloat16 or wider, within the bound.
A program may use at most 64 MiB of HBM per device.

```python
import jax
import jax.numpy as jnp
from jax import lax

FREQUENCY_BINS = 1024
LAGS = 1024
P_DEV = 256
PCOL = 512
NPAIR = 16384
S = 2048
CAP = 64
STACK_SLOT_COUNT = 32768
N_TM = 16
N_STA = 32


def draw_pair_list(key, part):
    keys = jax.random.split(key, N_TM * N_STA)
    picked = jax.vmap(lambda single: jax.random.permutation(single, PCOL)[:P_DEV])(keys)
    return picked.reshape(N_TM, N_STA, P_DEV).astype(jnp.int32)


def draw_owner_code(key, part):
    keys = jax.random.split(jax.random.fold_in(key, 7), N_STA)

    def single_column(single):
        first_key, second_key, tertiary_key = jax.random.split(single, 3)
        complete_owner = jax.random.randint(first_key, (), 0, N_TM)
        codes_all = jnp.arange(N_TM * CAP, dtype=jnp.int32)
        ranking = jax.random.permutation(second_key, N_TM * CAP).astype(jnp.int32)
        forced = (codes_all // CAP == complete_owner) | (codes_all == 0) | (codes_all == N_TM * CAP - 1)
        score = jnp.where(forced, 0, 1 + ranking)
        chosen = codes_all[jnp.argsort(score, stable=True)][:PCOL]
        return jax.random.permutation(tertiary_key, chosen)
    return jax.vmap(single_column)(keys).reshape(-1).astype(jnp.int32)


def with_ends(entries, own_key, smallest, largest):
    shape = entries.shape
    spot = [jax.random.randint(jax.random.fold_in(own_key, axis), (), 0, shape[axis]) for axis in range(len(shape))]
    entries = entries.at[tuple(spot)].set(smallest)
    longest = shape.index(max(shape))
    spot[longest] = (spot[longest] + 1) % shape[longest]
    return entries.at[tuple(spot)].set(largest)


def shard_levels(own_key, extent, cuts, smallest, high):
    factor_of = 1.0
    for axis_at, shards_of in cuts:
        draws = jax.random.uniform(jax.random.fold_in(jax.random.fold_in(own_key, 6), axis_at), (shards_of,), jnp.float32, smallest / len(cuts), high / len(cuts))
        factor_of = factor_of * jnp.repeat(jnp.exp(draws), extent[axis_at] // shards_of).reshape((-1,) + (1,) * (len(extent) - 1 - axis_at))
    return factor_of


def gaussian(own_key, shape, deviation, limit, shards=(), kind=jnp.bfloat16):
    entries = deviation * jax.random.normal(own_key, shape, jnp.float32)
    if shards:
        entries = entries * shard_levels(own_key, shape, shards, -0.22, 0.18)
    return jnp.clip(entries, -limit, limit).astype(kind)


def setup_inputs(seed: int = 0) -> dict:
    seeds = jax.random.split(jax.random.key(seed), 5)
    return {
        "spectra": gaussian(seeds[0], (N_TM, S, 2 * FREQUENCY_BINS), 0.7, 5.0, ((0, 16), (1, 32))),
        "pair_list": draw_pair_list(jax.random.fold_in(seeds[4], 71), 0),
        "pair_stations": with_ends(jax.random.randint(seeds[2], (2, NPAIR), 0, S), jax.random.fold_in(seeds[2], 1), 0, S - 1).astype(jnp.int32),
        "owner_code": draw_owner_code(jax.random.fold_in(seeds[4], 71), 0),
    }


def lag_table(bins, lags):
    bin_index = jnp.arange(bins, dtype=jnp.int32)[:, None]
    lag_index = jnp.arange(lags, dtype=jnp.int32)[None, :] - lags // 2
    phase = ((bin_index * lag_index) % (2 * bins)).astype(jnp.float32) * (jnp.pi / bins)
    scale = 1.0 / (bins ** 0.5)
    return jnp.concatenate([jnp.cos(phase) * scale, -jnp.sin(phase) * scale], axis=0)


def cross_spectra(first, second, bins):
    first = first.astype(jnp.float32)
    second = second.astype(jnp.float32)
    real_a, imag_a = first[..., :bins], first[..., bins:]
    real_b, imag_b = second[..., :bins], second[..., bins:]
    real_c = real_a * real_b + imag_a * imag_b
    imag_c = real_a * imag_b - imag_a * real_b
    return jnp.concatenate([real_c, imag_c], axis=-1)


def reference(spectra, pair_list, pair_stations, owner_code):
    column_entry = jnp.arange(N_STA, dtype=jnp.int32)[:, None]

    def single_group(group, running_totals):
        listed = pair_list[group] + column_entry * PCOL
        first = spectra[group][pair_stations[0][listed]]
        second = spectra[group][pair_stations[1][listed]]
        cross = cross_spectra(first, second, FREQUENCY_BINS)
        codes = owner_code[listed]
        rows = (codes // CAP) * (N_STA * CAP) + column_entry * CAP + codes % CAP
        return running_totals.at[rows.reshape(-1)].add(cross.reshape(-1, 2 * FREQUENCY_BINS))

    running_totals = lax.fori_loop(0, N_TM, single_group, jnp.zeros((STACK_SLOT_COUNT, 2 * FREQUENCY_BINS), jnp.float32))
    return jnp.dot(running_totals, lag_table(FREQUENCY_BINS, LAGS), precision=lax.Precision.HIGHEST, preferred_element_type=jnp.float32)
```

```python
import functools

import jax
import jax.numpy as jnp
from jax import lax
from jax.experimental import pallas as pl
from jax.experimental.pallas import tpu as pltpu
from jax.sharding import PartitionSpec as P

LAGS = 1024
NX, NZ, NY = 4, 8, 8
MESH = pl.DeviceIdType.MESH


def place(axis):
    sta = lax.axis_index("sta")
    tm = lax.axis_index("tm")
    x, z = lax.rem(sta, NX), lax.div(sta, NX)
    y, core = lax.div(tm, 2), lax.rem(tm, 2)
    if axis == "z":
        return z, NZ, lambda j: {"sta": j * NX + x}
    if axis == "x":
        return x, NX, lambda j: {"sta": z * NX + j}
    if axis == "tm":
        return tm, 2 * NY, lambda j: {"tm": j}
    if axis == "y":
        return y, NY, lambda j: {"tm": j * 2 + core}
    return core, 2, lambda j: {"tm": y * 2 + j}


def exchange_kernel(axis, modes, *refs):
    count = len(modes)
    ins, outs = refs[:count], refs[count : 2 * count]
    send_sem, recv_sem, own_sem = refs[2 * count :]
    me, size, peer = place(axis)
    barrier = pltpu.get_barrier_semaphore()
    for k in range(1, size):
        pl.semaphore_signal(
            barrier, inc=1, device_id=peer(lax.rem(me + k, size)), device_id_type=MESH
        )
    owns = []
    for i, mode in enumerate(modes):
        own = pltpu.make_async_copy(
            ins[i].at[me] if mode == "swap" else ins[i], outs[i].at[me], own_sem.at[i]
        )
        own.start()
        owns.append(own)
    pl.semaphore_wait(barrier, size - 1)
    sends = []
    for k in range(1, size):
        to = lax.rem(me + k, size)
        for i, mode in enumerate(modes):
            copy = pltpu.make_async_remote_copy(
                src_ref=ins[i].at[to] if mode == "swap" else ins[i],
                dst_ref=outs[i].at[me],
                send_sem=send_sem.at[i, k],
                recv_sem=recv_sem.at[i, k],
                device_id=peer(to),
                device_id_type=MESH,
            )
            copy.start()
            sends.append((copy, i, k))
    for copy, i, k in sends:
        copy.wait_send()
    for copy, i, k in sends:
        origin = lax.rem(me + size - k, size)
        pltpu.make_async_remote_copy(
            src_ref=outs[i].at[origin],
            dst_ref=outs[i].at[origin],
            send_sem=send_sem.at[i, k],
            recv_sem=recv_sem.at[i, k],
            device_id=peer(origin),
            device_id_type=MESH,
        ).wait_recv()
    for own in owns:
        own.wait()


def exchange(axis, identity, *pairs):
    size = {"z": NZ, "x": NX, "tm": 2 * NY, "y": NY, "core": 2}[axis]
    modes = tuple(mode for mode, _ in pairs)
    arrays = [array for _, array in pairs]
    shapes = [
        jax.ShapeDtypeStruct(
            array.shape if mode == "swap" else (size,) + array.shape, array.dtype
        )
        for mode, array in pairs
    ]
    count = len(pairs)
    vmem = pl.BlockSpec(memory_space=pltpu.VMEM)
    return pl.pallas_call(
        functools.partial(exchange_kernel, axis, modes),
        out_shape=shapes,
        in_specs=[vmem] * count,
        out_specs=[vmem] * count,
        scratch_shapes=[
            pltpu.SemaphoreType.DMA((count, size)),
            pltpu.SemaphoreType.DMA((count, size)),
            pltpu.SemaphoreType.DMA((count,)),
        ],
        compiler_params=pltpu.CompilerParams(
            collective_id=identity, has_side_effects=True
        ),
        name=f"exchange_{axis}",
    )(*arrays)


def stack_kernel(index_ref, mask_ref, data_ref, out_ref):
    first = index_ref[0, 0:1, :]
    second = index_ref[0, 1:2, :]
    code = index_ref[0, 2:3, :]
    pairs = first.shape[1]
    block = data_ref.shape[2]

    def pick(rows):
        total = None
        for part in range(data_ref.shape[0]):
            lane = lax.broadcasted_iota(jnp.int32, (block, pairs), 0) + part * block
            chosen = jnp.where(lane == rows, 1.0, 0.0).astype(jnp.bfloat16)
            term = jnp.dot(data_ref[part], chosen, preferred_element_type=jnp.float32)
            total = term if total is None else total + term
        return total.reshape(total.shape[0] // 16, 2, 8, pairs)

    a = pick(first)
    b = pick(second)
    mask = mask_ref[0].astype(jnp.float32)[:, None, :]
    real = jnp.sum((a[:, 0] * b[:, 0] + a[:, 1] * b[:, 1]) * mask, axis=0)
    imag = jnp.sum((a[:, 0] * b[:, 1] - a[:, 1] * b[:, 0]) * mask, axis=0)
    value = jnp.concatenate([real, imag], axis=0)
    high = value.astype(jnp.bfloat16)
    low = (value - high.astype(jnp.float32)).astype(jnp.bfloat16)
    slots = out_ref.shape[2]
    slot = lax.broadcasted_iota(jnp.int32, (slots, pairs), 0)
    chosen = jnp.where(slot == code, 1.0, 0.0).astype(jnp.bfloat16)
    contract = (((1,), (1,)), ((), ()))
    out_ref[0] = lax.dot_general(
        high, chosen, contract, preferred_element_type=jnp.float32
    ) + lax.dot_general(low, chosen, contract, preferred_element_type=jnp.float32)


def angles(bins, scale_bins):
    lag = jnp.arange(LAGS, dtype=jnp.int32)[None, :] - LAGS // 2
    phase = (bins[:, None] * lag) % (2 * scale_bins)
    phase = phase.astype(jnp.float32) * (jnp.pi / scale_bins)
    return jnp.cos(phase), jnp.sin(phase)


def half_table(bins):
    core = lax.axis_index("tm") % 2
    coarse = jnp.arange(NZ, dtype=jnp.int32) * (bins // NZ)
    number = jnp.arange(NY * 8, dtype=jnp.int32)
    fine = (number // 8 * 2 + core) * 8 + number % 8
    cos_c, sin_c = angles(coarse, bins)
    cos_f, sin_f = angles(fine, bins)
    scale = 1.0 / bins**0.5
    cos_c, sin_c = (cos_c * scale)[None, :, None], (sin_c * scale)[None, :, None]
    cos_f, sin_f = cos_f.reshape(NY, 1, 8, LAGS), sin_f.reshape(NY, 1, 8, LAGS)
    real = cos_c * cos_f - sin_c * sin_f
    imag = -(sin_c * cos_f + cos_c * sin_f)
    return jnp.stack([real, imag], axis=2).reshape(bins, LAGS)


def local(spectra, pair_list, pair_stations, owner_code):
    stations, width = spectra.shape[1:]
    bins = width // 2
    catalogue = owner_code.shape[0]
    groups = 2 * NY
    slots = 2 * catalogue
    f = bins // (NZ * groups)
    table = half_table(bins)
    shard, inner = pair_stations // stations, pair_stations % stations
    column = (shard % NX) * (NZ * stations) + (shard // NX) * stations + inner
    number = jnp.arange(catalogue, dtype=jnp.int32)
    listed = jnp.any(number[:, None] == pair_list[0, 0][None, :], axis=1)
    index = jnp.concatenate(
        [
            column,
            owner_code[None],
            listed.astype(jnp.int32)[None],
            jnp.zeros((4, catalogue), jnp.int32),
        ]
    )
    blocks = spectra[0].reshape(stations, 2, NZ, bins // NZ).transpose(2, 0, 1, 3)
    blocks = blocks.reshape(NZ, stations, 2 * bins // NZ)
    blocks, index = exchange("z", 0, ("swap", blocks), ("copy", index))
    mask = index[:, 3, :].astype(jnp.bfloat16).reshape(16, NZ * catalogue // 16)
    turned = blocks.reshape(NZ * stations, 2, groups, f).transpose(2, 1, 3, 0)
    turned = turned.reshape(groups, 2 * f, NZ * stations)
    turned, mask = exchange("tm", 1, ("swap", turned), ("copy", mask))
    (data,) = exchange("x", 2, ("copy", turned.reshape(groups * 2 * f, NZ * stations)))
    mask = mask.reshape(groups, NZ, catalogue).transpose(1, 0, 2)
    stacked = pl.pallas_call(
        stack_kernel,
        grid=(NZ,),
        out_shape=jax.ShapeDtypeStruct((NZ, 2 * f, slots), jnp.float32),
        in_specs=[
            pl.BlockSpec((1, 8, catalogue), lambda c: (c, 0, 0)),
            pl.BlockSpec((1, groups, catalogue), lambda c: (c, 0, 0)),
            pl.BlockSpec(data.shape, lambda c: (0, 0, 0)),
        ],
        out_specs=pl.BlockSpec((1, 2 * f, slots), lambda c: (c, 0, 0)),
        name="stack_pairs",
    )(index, mask, data)
    (stacked,) = exchange("z", 3, ("swap", stacked))
    stacked = stacked.reshape(NZ * 2 * f, NY, slots // NY).transpose(1, 0, 2)
    (stacked,) = exchange("y", 4, ("swap", stacked))
    halves = lax.dot_general(
        stacked.reshape(bins, slots // NY),
        table,
        (((0,), (0,)), ((), ())),
        precision=lax.Precision.HIGHEST,
        preferred_element_type=jnp.float32,
    )
    (halves,) = exchange("core", 5, ("swap", halves.reshape(2, slots // groups, LAGS)))
    return halves[0] + halves[1]


def solution(mesh):
    return jax.shard_map(
        local,
        mesh=mesh,
        in_specs=(P("tm", "sta", None), P("tm", "sta", None), P(None, "sta"), P("sta")),
        out_specs=P(("tm", "sta"), None),
        check_vma=False,
    )
```

```python
import functools

import jax
import jax.numpy as jnp
from jax import lax
from jax.experimental import pallas as pl
from jax.experimental.pallas import tpu as pltpu
from jax.sharding import PartitionSpec as P

LAGS = 1024
NX, NZ, NY = 4, 8, 8
MESH = pl.DeviceIdType.MESH


def place(axis):
    sta = lax.axis_index("sta")
    tm = lax.axis_index("tm")
    x, z = lax.rem(sta, NX), lax.div(sta, NX)
    y, core = lax.div(tm, 2), lax.rem(tm, 2)
    if axis == "z":
        return z, NZ, lambda j: {"sta": j * NX + x}
    if axis == "x":
        return x, NX, lambda j: {"sta": z * NX + j}
    if axis == "tm":
        return tm, 2 * NY, lambda j: {"tm": j}
    if axis == "y":
        return y, NY, lambda j: {"tm": j * 2 + core}
    return core, 2, lambda j: {"tm": y * 2 + j}


def exchange_kernel(axis, modes, *refs):
    count = len(modes)
    ins, outs = refs[:count], refs[count : 2 * count]
    send_sem, recv_sem, own_sem = refs[2 * count :]
    me, size, peer = place(axis)
    barrier = pltpu.get_barrier_semaphore()
    for k in range(1, size):
        pl.semaphore_signal(
            barrier, inc=1, device_id=peer(lax.rem(me + k, size)), device_id_type=MESH
        )
    owns = []
    for i, mode in enumerate(modes):
        own = pltpu.make_async_copy(
            ins[i].at[me] if mode == "swap" else ins[i], outs[i].at[me], own_sem.at[i]
        )
        own.start()
        owns.append(own)
    pl.semaphore_wait(barrier, size - 1)
    sends = []
    for k in range(1, size):
        to = lax.rem(me + k, size)
        for i, mode in enumerate(modes):
            copy = pltpu.make_async_remote_copy(
                src_ref=ins[i].at[to] if mode == "swap" else ins[i],
                dst_ref=outs[i].at[me],
                send_sem=send_sem.at[i, k],
                recv_sem=recv_sem.at[i, k],
                device_id=peer(to),
                device_id_type=MESH,
            )
            copy.start()
            sends.append((copy, i, k))
    for copy, i, k in sends:
        copy.wait_send()
    for copy, i, k in sends:
        origin = lax.rem(me + size - k, size)
        pltpu.make_async_remote_copy(
            src_ref=outs[i].at[origin],
            dst_ref=outs[i].at[origin],
            send_sem=send_sem.at[i, k],
            recv_sem=recv_sem.at[i, k],
            device_id=peer(origin),
            device_id_type=MESH,
        ).wait_recv()
    for own in owns:
        own.wait()


def greet(groups):
    barrier = pltpu.get_barrier_semaphore()
    for me, size, peer in groups:
        for k in range(1, size):
            pl.semaphore_signal(
                barrier, inc=1, device_id=peer(lax.rem(me + k, size)), device_id_type=MESH
            )
    return barrier, sum(size - 1 for _, size, _ in groups)


def remote(src, dst, send_sem, recv_sem, device):
    return pltpu.make_async_remote_copy(
        src_ref=src,
        dst_ref=dst,
        send_sem=send_sem,
        recv_sem=recv_sem,
        device_id=device,
        device_id_type=MESH,
    )


def turn_kernel(
    block_ref, mask_ref, data_ref, masks_ref,
    t_send, t_recv, m_send, m_recv, x_send, x_recv, own_sem,
):
    me, size, peer = place("tm")
    x, wide, beside = place("x")
    barrier, count = greet([(me, size, peer), (x, wide, beside)])
    own = pltpu.make_async_copy(block_ref.at[me], data_ref.at[x, me], own_sem.at[0])
    own_mask = pltpu.make_async_copy(mask_ref, masks_ref.at[me], own_sem.at[1])
    own.start()
    own_mask.start()
    pl.semaphore_wait(barrier, count)
    order = sorted(range(1, size), key=lambda k: min(k, size - k))
    pending = []

    def forward(k, src, group):
        for j in range(1, wide):
            copy = remote(
                src,
                data_ref.at[x, group],
                x_send.at[k, j],
                x_recv.at[k, j],
                beside(lax.rem(x + j, wide)),
            )
            copy.start()
            pending.append(copy)

    for k in order:
        to = lax.rem(me + k, size)
        copy = remote(
            block_ref.at[to], data_ref.at[x, me], t_send.at[k], t_recv.at[k], peer(to)
        )
        copy.start()
        pending.append(copy)
    forward(0, block_ref.at[me], me)
    for k in order:
        to = lax.rem(me + k, size)
        copy = remote(mask_ref, masks_ref.at[me], m_send.at[k], m_recv.at[k], peer(to))
        copy.start()
        pending.append(copy)
    for k in order:
        origin = lax.rem(me + size - k, size)
        landed = data_ref.at[x, origin]
        remote(landed, landed, t_send.at[k], t_recv.at[k], peer(origin)).wait_recv()
        forward(k, landed, origin)
    for k in order:
        origin = lax.rem(me + size - k, size)
        landed = masks_ref.at[origin]
        remote(landed, landed, m_send.at[k], m_recv.at[k], peer(origin)).wait_recv()
    for k in [0] + order:
        group = lax.rem(me + size - k, size)
        for j in range(1, wide):
            origin = lax.rem(x + wide - j, wide)
            landed = data_ref.at[origin, group]
            remote(
                landed, landed, x_send.at[k, j], x_recv.at[k, j], beside(origin)
            ).wait_recv()
    for copy in pending:
        copy.wait_send()
    own.wait()
    own_mask.wait()


def turn(blocks, mask):
    size = 2 * NY
    vmem = pl.BlockSpec(memory_space=pltpu.VMEM)
    dma = pltpu.SemaphoreType.DMA
    return pl.pallas_call(
        turn_kernel,
        out_shape=[
            jax.ShapeDtypeStruct((NX,) + blocks.shape, blocks.dtype),
            jax.ShapeDtypeStruct((size,) + mask.shape, mask.dtype),
        ],
        in_specs=[vmem] * 2,
        out_specs=[vmem] * 2,
        scratch_shapes=[dma((size,))] * 4 + [dma((size, NX))] * 2 + [dma((2,))],
        compiler_params=pltpu.CompilerParams(collective_id=1, has_side_effects=True),
        name="turn",
    )(blocks, mask)


def exchange(axis, identity, *pairs):
    size = {"z": NZ, "x": NX, "tm": 2 * NY, "y": NY, "core": 2}[axis]
    modes = tuple(mode for mode, _ in pairs)
    arrays = [array for _, array in pairs]
    shapes = [
        jax.ShapeDtypeStruct(
            array.shape if mode == "swap" else (size,) + array.shape, array.dtype
        )
        for mode, array in pairs
    ]
    count = len(pairs)
    vmem = pl.BlockSpec(memory_space=pltpu.VMEM)
    return pl.pallas_call(
        functools.partial(exchange_kernel, axis, modes),
        out_shape=shapes,
        in_specs=[vmem] * count,
        out_specs=[vmem] * count,
        scratch_shapes=[
            pltpu.SemaphoreType.DMA((count, size)),
            pltpu.SemaphoreType.DMA((count, size)),
            pltpu.SemaphoreType.DMA((count,)),
        ],
        compiler_params=pltpu.CompilerParams(
            collective_id=identity, has_side_effects=True
        ),
        name=f"exchange_{axis}",
    )(*arrays)


def stack_one(index_ref, mask_ref, data_ref, result_ref, c):
    first = index_ref[c, 0:1, :]
    second = index_ref[c, 1:2, :]
    code = index_ref[c, 2:3, :]
    pairs = first.shape[1]
    block = data_ref.shape[2]

    def pick(rows):
        total = None
        for part in range(data_ref.shape[0]):
            lane = lax.broadcasted_iota(jnp.int32, (block, pairs), 0) + part * block
            chosen = jnp.where(lane == rows, 1.0, 0.0).astype(jnp.bfloat16)
            term = jnp.dot(data_ref[part], chosen, preferred_element_type=jnp.float32)
            total = term if total is None else total + term
        return total.reshape(total.shape[0] // 16, 2, 8, pairs)

    a = pick(first)
    b = pick(second)
    mask = mask_ref[c][:, None, :]
    real = jnp.sum((a[:, 0] * b[:, 0] + a[:, 1] * b[:, 1]) * mask, axis=0)
    imag = jnp.sum((a[:, 0] * b[:, 1] - a[:, 1] * b[:, 0]) * mask, axis=0)
    value = jnp.concatenate([real, imag], axis=0)
    high = value.astype(jnp.bfloat16)
    low = (value - high.astype(jnp.float32)).astype(jnp.bfloat16)
    slots = result_ref.shape[2]
    slot = lax.broadcasted_iota(jnp.int32, (slots, pairs), 0)
    chosen = jnp.where(slot == code, 1.0, 0.0).astype(jnp.bfloat16)
    contract = (((1,), (1,)), ((), ()))
    result_ref[c] = lax.dot_general(
        high, chosen, contract, preferred_element_type=jnp.float32
    ) + lax.dot_general(low, chosen, contract, preferred_element_type=jnp.float32)


def stack_kernel(
    index_ref, mask_ref, data_ref, out_ref,
    result_ref, landed_ref, z_send, z_recv, y_send, y_recv, own_sem,
):
    z, deep, along = place("z")
    y, tall, above = place("y")
    width = out_ref.shape[3]
    barrier, count = greet([(z, deep, along), (y, tall, above)])

    def compute(k):
        stack_one(index_ref, mask_ref, data_ref, result_ref, lax.rem(z + k, deep))

    def send(k):
        to = lax.rem(z + k, deep)
        return remote(
            result_ref.at[to], landed_ref.at[z], z_send.at[k], z_recv.at[k], along(to)
        )

    def lanes(j):
        return pl.ds(pl.multiple_of(j * width, width), width)

    def share(k, origin, src_ref):
        own = pltpu.make_async_copy(
            src_ref.at[origin, :, lanes(y)], out_ref.at[y, origin], own_sem.at[k]
        )
        away = []
        for j in range(1, tall):
            to = lax.rem(y + j, tall)
            away.append(
                remote(
                    src_ref.at[origin, :, lanes(to)],
                    out_ref.at[y, origin],
                    y_send.at[k, j],
                    y_recv.at[k, j],
                    above(to),
                )
            )
        return own, away

    def forward(k, origin, src_ref):
        own, away = share(k, origin, src_ref)
        own.start()
        for copy in away:
            copy.start()

    def receive(k):
        origin = lax.rem(z + deep - k, deep)
        landed = landed_ref.at[origin]
        remote(landed, landed, z_send.at[k], z_recv.at[k], along(origin)).wait_recv()
        forward(k, origin, landed_ref)

    compute(0)
    pl.semaphore_wait(barrier, count)

    @pl.loop(1, deep)
    def _(k):
        compute(k)

        @pl.when(k == 1)
        def _():
            forward(0, z, result_ref)

        @pl.when(k >= 2)
        def _():
            send(k - 1).start()

        @pl.when(k >= 3)
        def _():
            receive(k - 2)

    send(deep - 1).start()
    receive(deep - 2)
    receive(deep - 1)
    for k in range(deep):
        if k:
            send(k).wait_send()
        origin = lax.rem(z + deep - k, deep)
        own, away = share(k, origin, landed_ref if k else result_ref)
        own.wait()
        for copy in away:
            copy.wait_send()
        for j in range(1, tall):
            below = lax.rem(y + tall - j, tall)
            arrived = out_ref.at[below, origin]
            remote(
                arrived, arrived, y_send.at[k, j], y_recv.at[k, j], above(below)
            ).wait_recv()


def stack_pairs(index, mask, data, slots):
    rows = 16
    vmem = pl.BlockSpec(memory_space=pltpu.VMEM)
    dma = pltpu.SemaphoreType.DMA
    return pl.pallas_call(
        stack_kernel,
        out_shape=jax.ShapeDtypeStruct((NY, NZ, rows, slots // NY), jnp.float32),
        in_specs=[vmem] * 3,
        out_specs=vmem,
        scratch_shapes=[pltpu.VMEM((NZ, rows, slots), jnp.float32)] * 2
        + [dma((NZ,))] * 2
        + [dma((NZ, NY))] * 2
        + [dma((NZ,))],
        compiler_params=pltpu.CompilerParams(collective_id=2, has_side_effects=True),
        name="stack_pairs",
    )(index, mask, data)


def angles(bins, scale_bins):
    lag = jnp.arange(LAGS, dtype=jnp.int32)[None, :] - LAGS // 2
    phase = (bins[:, None] * lag) % (2 * scale_bins)
    phase = phase.astype(jnp.float32) * (jnp.pi / scale_bins)
    return jnp.cos(phase), jnp.sin(phase)


def half_table(bins):
    core = lax.axis_index("tm") % 2
    coarse = jnp.arange(NZ, dtype=jnp.int32) * (bins // NZ)
    number = jnp.arange(NY * 8, dtype=jnp.int32)
    fine = (number // 8 * 2 + core) * 8 + number % 8
    cos_c, sin_c = angles(coarse, bins)
    cos_f, sin_f = angles(fine, bins)
    scale = 1.0 / bins**0.5
    cos_c, sin_c = (cos_c * scale)[None, :, None], (sin_c * scale)[None, :, None]
    cos_f, sin_f = cos_f.reshape(NY, 1, 8, LAGS), sin_f.reshape(NY, 1, 8, LAGS)
    real = cos_c * cos_f - sin_c * sin_f
    imag = -(sin_c * cos_f + cos_c * sin_f)
    return jnp.stack([real, imag], axis=2).reshape(bins, LAGS)


def local(spectra, pair_list, pair_stations, owner_code):
    stations, width = spectra.shape[1:]
    bins = width // 2
    catalogue = owner_code.shape[0]
    groups = 2 * NY
    slots = 2 * catalogue
    f = bins // (NZ * groups)
    table = half_table(bins)
    shard, inner = pair_stations // stations, pair_stations % stations
    column = (shard % NX) * (NZ * stations) + (shard // NX) * stations + inner
    number = jnp.arange(catalogue, dtype=jnp.int32)
    listed = jnp.any(number[:, None] == pair_list[0, 0][None, :], axis=1)
    index = jnp.concatenate(
        [
            column,
            owner_code[None],
            listed.astype(jnp.int32)[None],
            jnp.zeros((4, catalogue), jnp.int32),
        ]
    )
    blocks = spectra[0].reshape(stations, 2, NZ, bins // NZ).transpose(2, 0, 1, 3)
    blocks = blocks.reshape(NZ, stations, 2 * bins // NZ)
    blocks, index = exchange("z", 0, ("swap", blocks), ("copy", index))
    mask = index[:, 3, :].astype(jnp.bfloat16)
    turned = blocks.reshape(NZ * stations, 2, groups, f).transpose(2, 1, 3, 0)
    data, mask = turn(turned.reshape(groups, 2 * f, NZ * stations), mask)
    data = data.reshape(NX, groups * 2 * f, NZ * stations)
    mask = mask.astype(jnp.float32).transpose(1, 0, 2)
    stacked = stack_pairs(index, mask, data, slots)
    halves = lax.dot_general(
        stacked.reshape(bins, slots // NY),
        table,
        (((0,), (0,)), ((), ())),
        precision=lax.Precision.HIGH,
        preferred_element_type=jnp.float32,
    )
    (halves,) = exchange("core", 3, ("swap", halves.reshape(2, slots // groups, LAGS)))
    return halves[0] + halves[1]


def solution(mesh):
    return jax.shard_map(
        local,
        mesh=mesh,
        in_specs=(P("tm", "sta", None), P("tm", "sta", None), P(None, "sta"), P("sta")),
        out_specs=P(("tm", "sta"), None),
        check_vma=False,
    )
```

```python
import functools

import jax
import jax.numpy as jnp
from jax import lax
from jax.experimental import pallas as pl
from jax.experimental.pallas import tpu as pltpu
from jax.sharding import PartitionSpec as P

LAGS = 1024
NX, NZ, NY = 4, 8, 8
MESH = pl.DeviceIdType.MESH


def place(axis):
    sta = lax.axis_index("sta")
    tm = lax.axis_index("tm")
    x, z = lax.rem(sta, NX), lax.div(sta, NX)
    y, core = lax.div(tm, 2), lax.rem(tm, 2)
    if axis == "z":
        return z, NZ, lambda j: {"sta": j * NX + x}
    if axis == "x":
        return x, NX, lambda j: {"sta": z * NX + j}
    if axis == "tm":
        return tm, 2 * NY, lambda j: {"tm": j}
    if axis == "y":
        return y, NY, lambda j: {"tm": j * 2 + core}
    return core, 2, lambda j: {"tm": y * 2 + j}


def exchange_kernel(axis, modes, *refs):
    count = len(modes)
    ins, outs = refs[:count], refs[count : 2 * count]
    send_sem, recv_sem, own_sem = refs[2 * count :]
    me, size, peer = place(axis)
    barrier = pltpu.get_barrier_semaphore()
    for k in range(1, size):
        pl.semaphore_signal(
            barrier, inc=1, device_id=peer(lax.rem(me + k, size)), device_id_type=MESH
        )
    owns = []
    for i, mode in enumerate(modes):
        own = pltpu.make_async_copy(
            ins[i].at[me] if mode == "swap" else ins[i], outs[i].at[me], own_sem.at[i]
        )
        own.start()
        owns.append(own)
    pl.semaphore_wait(barrier, size - 1)
    sends = []
    for k in range(1, size):
        to = lax.rem(me + k, size)
        for i, mode in enumerate(modes):
            copy = pltpu.make_async_remote_copy(
                src_ref=ins[i].at[to] if mode == "swap" else ins[i],
                dst_ref=outs[i].at[me],
                send_sem=send_sem.at[i, k],
                recv_sem=recv_sem.at[i, k],
                device_id=peer(to),
                device_id_type=MESH,
            )
            copy.start()
            sends.append((copy, i, k))
    for copy, i, k in sends:
        copy.wait_send()
    for copy, i, k in sends:
        origin = lax.rem(me + size - k, size)
        pltpu.make_async_remote_copy(
            src_ref=outs[i].at[origin],
            dst_ref=outs[i].at[origin],
            send_sem=send_sem.at[i, k],
            recv_sem=recv_sem.at[i, k],
            device_id=peer(origin),
            device_id_type=MESH,
        ).wait_recv()
    for own in owns:
        own.wait()


def greet(groups):
    barrier = pltpu.get_barrier_semaphore()
    for me, size, peer in groups:
        for k in range(1, size):
            pl.semaphore_signal(
                barrier, inc=1, device_id=peer(lax.rem(me + k, size)), device_id_type=MESH
            )
    return barrier, sum(size - 1 for _, size, _ in groups)


def remote(src, dst, send_sem, recv_sem, device):
    return pltpu.make_async_remote_copy(
        src_ref=src,
        dst_ref=dst,
        send_sem=send_sem,
        recv_sem=recv_sem,
        device_id=device,
        device_id_type=MESH,
    )


def turn_kernel(
    block_ref, mask_ref, data_ref, masks_ref,
    t_send, t_recv, m_send, m_recv, x_send, x_recv, own_sem,
):
    me, size, peer = place("tm")
    x, wide, beside = place("x")
    barrier, count = greet([(me, size, peer), (x, wide, beside)])
    own = pltpu.make_async_copy(block_ref.at[me], data_ref.at[x, me], own_sem.at[0])
    own_mask = pltpu.make_async_copy(mask_ref, masks_ref.at[me], own_sem.at[1])
    own.start()
    own_mask.start()
    pl.semaphore_wait(barrier, count)
    order = sorted(range(1, size), key=lambda k: min(k, size - k))
    pending = []

    def step_x(k, j, src, owner, group, by):
        copy = remote(
            src,
            data_ref.at[owner, group],
            x_send.at[k, j],
            x_recv.at[k, j],
            beside(lax.rem(x + by, wide)),
        )
        copy.start()
        pending.append(copy)

    def forward(k, src, group):
        step_x(k, 1, src, x, group, 1)
        step_x(k, 3, src, x, group, wide - 1)

    def land_x(k, j, group):
        origin = lax.rem(x + wide - j, wide)
        landed = data_ref.at[origin, group]
        remote(landed, landed, x_send.at[k, j], x_recv.at[k, j], beside(origin)).wait_recv()
        return origin, landed

    for k in order:
        to = lax.rem(me + k, size)
        copy = remote(
            block_ref.at[to], data_ref.at[x, me], t_send.at[k], t_recv.at[k], peer(to)
        )
        copy.start()
        pending.append(copy)
    forward(0, block_ref.at[me], me)
    for k in order:
        to = lax.rem(me + k, size)
        copy = remote(mask_ref, masks_ref.at[me], m_send.at[k], m_recv.at[k], peer(to))
        copy.start()
        pending.append(copy)
    for k in order:
        origin = lax.rem(me + size - k, size)
        landed = data_ref.at[x, origin]
        remote(landed, landed, t_send.at[k], t_recv.at[k], peer(origin)).wait_recv()
        forward(k, landed, origin)
    for k in order:
        origin = lax.rem(me + size - k, size)
        landed = masks_ref.at[origin]
        remote(landed, landed, m_send.at[k], m_recv.at[k], peer(origin)).wait_recv()
    for n, k in enumerate([0] + order):
        group = lax.rem(me + size - k, size)
        for j in (1, 3):
            origin, landed = land_x(k, j, group)
            if (j == 1) == (n % 4 in (0, 3)):
                step_x(k, 2, landed, origin, group, j)
    for k in [0] + order:
        land_x(k, 2, lax.rem(me + size - k, size))
    for copy in pending:
        copy.wait_send()
    own.wait()
    own_mask.wait()


def turn(blocks, mask):
    size = 2 * NY
    vmem = pl.BlockSpec(memory_space=pltpu.VMEM)
    dma = pltpu.SemaphoreType.DMA
    return pl.pallas_call(
        turn_kernel,
        out_shape=[
            jax.ShapeDtypeStruct((NX,) + blocks.shape, blocks.dtype),
            jax.ShapeDtypeStruct((size,) + mask.shape, mask.dtype),
        ],
        in_specs=[vmem] * 2,
        out_specs=[vmem] * 2,
        scratch_shapes=[dma((size,))] * 4 + [dma((size, NX))] * 2 + [dma((2,))],
        compiler_params=pltpu.CompilerParams(collective_id=1, has_side_effects=True),
        name="turn",
    )(blocks, mask)


def exchange(axis, identity, *pairs):
    size = {"z": NZ, "x": NX, "tm": 2 * NY, "y": NY, "core": 2}[axis]
    modes = tuple(mode for mode, _ in pairs)
    arrays = [array for _, array in pairs]
    shapes = [
        jax.ShapeDtypeStruct(
            array.shape if mode == "swap" else (size,) + array.shape, array.dtype
        )
        for mode, array in pairs
    ]
    count = len(pairs)
    vmem = pl.BlockSpec(memory_space=pltpu.VMEM)
    return pl.pallas_call(
        functools.partial(exchange_kernel, axis, modes),
        out_shape=shapes,
        in_specs=[vmem] * count,
        out_specs=[vmem] * count,
        scratch_shapes=[
            pltpu.SemaphoreType.DMA((count, size)),
            pltpu.SemaphoreType.DMA((count, size)),
            pltpu.SemaphoreType.DMA((count,)),
        ],
        compiler_params=pltpu.CompilerParams(
            collective_id=identity, has_side_effects=True
        ),
        name=f"exchange_{axis}",
    )(*arrays)


def stack_one(index_ref, mask_ref, data_ref, result_ref, c):
    first = index_ref[c, 0:1, :]
    second = index_ref[c, 1:2, :]
    code = index_ref[c, 2:3, :]
    pairs = first.shape[1]
    block = data_ref.shape[2]

    def pick(rows):
        total = None
        for part in range(data_ref.shape[0]):
            lane = lax.broadcasted_iota(jnp.int32, (block, pairs), 0) + part * block
            chosen = jnp.where(lane == rows, 1.0, 0.0).astype(jnp.bfloat16)
            term = jnp.dot(data_ref[part], chosen, preferred_element_type=jnp.float32)
            total = term if total is None else total + term
        return total.reshape(total.shape[0] // 16, 2, 8, pairs)

    a = pick(first)
    b = pick(second)
    mask = mask_ref[c][:, None, :]
    real = jnp.sum((a[:, 0] * b[:, 0] + a[:, 1] * b[:, 1]) * mask, axis=0)
    imag = jnp.sum((a[:, 0] * b[:, 1] - a[:, 1] * b[:, 0]) * mask, axis=0)
    value = jnp.concatenate([real, imag], axis=0)
    high = value.astype(jnp.bfloat16)
    low = (value - high.astype(jnp.float32)).astype(jnp.bfloat16)
    slots = result_ref.shape[2]
    slot = lax.broadcasted_iota(jnp.int32, (slots, pairs), 0)
    chosen = jnp.where(slot == code, 1.0, 0.0).astype(jnp.bfloat16)
    contract = (((1,), (1,)), ((), ()))
    result_ref[c] = lax.dot_general(
        high, chosen, contract, preferred_element_type=jnp.float32
    ) + lax.dot_general(low, chosen, contract, preferred_element_type=jnp.float32)


def stack_kernel(
    index_ref, mask_ref, data_ref, out_ref,
    result_ref, landed_ref, z_send, z_recv, y_send, y_recv, own_sem,
):
    z, deep, along = place("z")
    y, tall, above = place("y")
    width = out_ref.shape[3]
    barrier, count = greet([(z, deep, along), (y, tall, above)])

    def compute(k):
        stack_one(index_ref, mask_ref, data_ref, result_ref, lax.rem(z + k, deep))

    def send(k):
        to = lax.rem(z + k, deep)
        return remote(
            result_ref.at[to], landed_ref.at[z], z_send.at[k], z_recv.at[k], along(to)
        )

    def lanes(j):
        return pl.ds(pl.multiple_of(j * width, width), width)

    def share(k, origin, src_ref):
        own = pltpu.make_async_copy(
            src_ref.at[origin, :, lanes(y)], out_ref.at[y, origin], own_sem.at[k]
        )
        away = []
        for j in range(1, tall):
            to = lax.rem(y + j, tall)
            away.append(
                remote(
                    src_ref.at[origin, :, lanes(to)],
                    out_ref.at[y, origin],
                    y_send.at[k, j],
                    y_recv.at[k, j],
                    above(to),
                )
            )
        return own, away

    def forward(k, origin, src_ref):
        own, away = share(k, origin, src_ref)
        own.start()
        for copy in away:
            copy.start()

    def receive(k):
        origin = lax.rem(z + deep - k, deep)
        landed = landed_ref.at[origin]
        remote(landed, landed, z_send.at[k], z_recv.at[k], along(origin)).wait_recv()
        forward(k, origin, landed_ref)

    def offset(step):
        return lax.rem(3 * step + 4, deep)

    compute(offset(0))
    pl.semaphore_wait(barrier, count)

    @pl.loop(1, deep)
    def _(step):
        compute(offset(step))

        @pl.when(step != 5)
        def _():
            send(offset(step - 1)).start()

        @pl.when(step == 4)
        def _():
            receive(7)

        @pl.when(step == 5)
        def _():
            forward(0, z, result_ref)

        @pl.when(step == 6)
        def _():
            receive(4)

        @pl.when(step == 7)
        def _():
            receive(2)

    send(1).start()
    for k in (5, 3, 6, 1):
        receive(k)
    for k in range(deep):
        if k:
            send(k).wait_send()
        origin = lax.rem(z + deep - k, deep)
        own, away = share(k, origin, landed_ref if k else result_ref)
        own.wait()
        for copy in away:
            copy.wait_send()
        for j in range(1, tall):
            below = lax.rem(y + tall - j, tall)
            arrived = out_ref.at[below, origin]
            remote(
                arrived, arrived, y_send.at[k, j], y_recv.at[k, j], above(below)
            ).wait_recv()


def stack_pairs(index, mask, data, slots):
    rows = 16
    vmem = pl.BlockSpec(memory_space=pltpu.VMEM)
    dma = pltpu.SemaphoreType.DMA
    return pl.pallas_call(
        stack_kernel,
        out_shape=jax.ShapeDtypeStruct((NY, NZ, rows, slots // NY), jnp.float32),
        in_specs=[vmem] * 3,
        out_specs=vmem,
        scratch_shapes=[pltpu.VMEM((NZ, rows, slots), jnp.float32)] * 2
        + [dma((NZ,))] * 2
        + [dma((NZ, NY))] * 2
        + [dma((NZ,))],
        compiler_params=pltpu.CompilerParams(collective_id=2, has_side_effects=True),
        name="stack_pairs",
    )(index, mask, data)


def lag_kernel(
    stacked_ref, high_ref, low_ref, out_ref, part_ref, landed_ref, send_sem, recv_sem
):
    core, size, peer = place("core")
    barrier, count = greet([(core, size, peer)])
    stacked = stacked_ref[...]
    high = stacked.astype(jnp.bfloat16)
    low = (stacked - high.astype(jnp.float32)).astype(jnp.bfloat16)
    chunks, rows, width = landed_ref.shape
    other = 1 - core

    def product(left, right):
        return lax.dot_general(
            left, right, (((0,), (0,)), ((), ())), preferred_element_type=jnp.float32
        )

    def copy(n):
        return remote(
            part_ref.at[n, pl.ds(pl.multiple_of(other * rows, rows), rows)],
            landed_ref.at[n],
            send_sem.at[n],
            recv_sem.at[n],
            peer(other),
        )

    for n in range(chunks):
        lags = pl.ds(n * width, width)
        part_ref[n] = (
            product(high, high_ref[:, lags])
            + product(high, low_ref[:, lags])
            + product(low, high_ref[:, lags])
        )
        if n == 0:
            pl.semaphore_wait(barrier, count)
        else:
            copy(n - 1).start()
    copy(chunks - 1).start()
    for n in range(chunks):
        copy(n).wait_recv()
        own = part_ref[n, pl.ds(pl.multiple_of(core * rows, rows), rows)]
        out_ref[:, pl.ds(n * width, width)] = own + landed_ref[n]
    for n in range(chunks):
        copy(n).wait_send()


def lag_product(stacked, high, low, chunks=4):
    rows = stacked.shape[1] // 2
    width = LAGS // chunks
    vmem = pl.BlockSpec(memory_space=pltpu.VMEM)
    dma = pltpu.SemaphoreType.DMA
    return pl.pallas_call(
        lag_kernel,
        out_shape=jax.ShapeDtypeStruct((rows, LAGS), jnp.float32),
        in_specs=[vmem] * 3,
        out_specs=vmem,
        scratch_shapes=[
            pltpu.VMEM((chunks, 2 * rows, width), jnp.float32),
            pltpu.VMEM((chunks, rows, width), jnp.float32),
            dma((chunks,)),
            dma((chunks,)),
        ],
        compiler_params=pltpu.CompilerParams(collective_id=3, has_side_effects=True),
        name="lag_product",
    )(stacked, high, low)


def angles(bins, scale_bins):
    lag = jnp.arange(LAGS, dtype=jnp.int32)[None, :] - LAGS // 2
    phase = (bins[:, None] * lag) % (2 * scale_bins)
    phase = phase.astype(jnp.float32) * (jnp.pi / scale_bins)
    return jnp.cos(phase), jnp.sin(phase)


def half_table(bins):
    core = lax.axis_index("tm") % 2
    coarse = jnp.arange(NZ, dtype=jnp.int32) * (bins // NZ)
    number = jnp.arange(NY * 8, dtype=jnp.int32)
    fine = (number // 8 * 2 + core) * 8 + number % 8
    cos_c, sin_c = angles(coarse, bins)
    cos_f, sin_f = angles(fine, bins)
    scale = 1.0 / bins**0.5
    cos_c, sin_c = (cos_c * scale)[None, :, None], (sin_c * scale)[None, :, None]
    cos_f, sin_f = cos_f.reshape(NY, 1, 8, LAGS), sin_f.reshape(NY, 1, 8, LAGS)
    real = cos_c * cos_f - sin_c * sin_f
    imag = -(sin_c * cos_f + cos_c * sin_f)
    return jnp.stack([real, imag], axis=2).reshape(bins, LAGS)


def local(spectra, pair_list, pair_stations, owner_code):
    stations, width = spectra.shape[1:]
    bins = width // 2
    catalogue = owner_code.shape[0]
    groups = 2 * NY
    slots = 2 * catalogue
    f = bins // (NZ * groups)
    table = half_table(bins)
    shard, inner = pair_stations // stations, pair_stations % stations
    column = (shard % NX) * (NZ * stations) + (shard // NX) * stations + inner
    number = jnp.arange(catalogue, dtype=jnp.int32)
    listed = jnp.any(number[:, None] == pair_list[0, 0][None, :], axis=1)
    index = jnp.concatenate(
        [
            column,
            owner_code[None],
            listed.astype(jnp.int32)[None],
        ]
    )
    blocks = spectra[0].reshape(stations, 2, NZ, bins // NZ).transpose(2, 0, 1, 3)
    blocks = blocks.reshape(NZ, stations, 2 * bins // NZ)
    blocks, index = exchange("z", 0, ("swap", blocks), ("copy", index))
    mask = index[:, 3, :].astype(jnp.bfloat16)
    turned = blocks.reshape(NZ * stations, 2, groups, f).transpose(2, 1, 3, 0)
    data, mask = turn(turned.reshape(groups, 2 * f, NZ * stations), mask)
    data = data.reshape(NX, groups * 2 * f, NZ * stations)
    mask = mask.astype(jnp.float32).transpose(1, 0, 2)
    stacked = stack_pairs(index, mask, data, slots)
    high = lax.reduce_precision(table, exponent_bits=8, mantissa_bits=7)
    low = (table - high).astype(jnp.bfloat16)
    high = high.astype(jnp.bfloat16)
    return lag_product(stacked.reshape(bins, slots // NY), high, low)


def solution(mesh):
    return jax.shard_map(
        local,
        mesh=mesh,
        in_specs=(P("tm", "sta", None), P("tm", "sta", None), P(None, "sta"), P("sta")),
        out_specs=P(("tm", "sta"), None),
        check_vma=False,
    )
```

```python
import functools

import jax
import jax.numpy as jnp
from jax import lax
from jax.experimental import pallas as pl
from jax.experimental.pallas import tpu as pltpu
from jax.sharding import PartitionSpec as P

LAGS = 1024
NX, NZ, NY = 4, 8, 8
MESH = pl.DeviceIdType.MESH


def place(axis):
    sta = lax.axis_index("sta")
    tm = lax.axis_index("tm")
    x, z = lax.rem(sta, NX), lax.div(sta, NX)
    y, core = lax.div(tm, 2), lax.rem(tm, 2)
    if axis == "z":
        return z, NZ, lambda j: {"sta": j * NX + x}
    if axis == "x":
        return x, NX, lambda j: {"sta": z * NX + j}
    if axis == "tm":
        return tm, 2 * NY, lambda j: {"tm": j}
    if axis == "y":
        return y, NY, lambda j: {"tm": j * 2 + core}
    return core, 2, lambda j: {"tm": y * 2 + j}


def exchange_kernel(axis, modes, *refs):
    count = len(modes)
    ins, outs = refs[:count], refs[count : 2 * count]
    send_sem, recv_sem, own_sem = refs[2 * count :]
    me, size, peer = place(axis)
    barrier = pltpu.get_barrier_semaphore()
    for k in range(1, size):
        pl.semaphore_signal(
            barrier, inc=1, device_id=peer(lax.rem(me + k, size)), device_id_type=MESH
        )
    owns = []
    for i, mode in enumerate(modes):
        own = pltpu.make_async_copy(
            ins[i].at[me] if mode == "swap" else ins[i], outs[i].at[me], own_sem.at[i]
        )
        own.start()
        owns.append(own)
    pl.semaphore_wait(barrier, size - 1)
    sends = []
    for k in range(1, size):
        to = lax.rem(me + k, size)
        for i, mode in enumerate(modes):
            copy = pltpu.make_async_remote_copy(
                src_ref=ins[i].at[to] if mode == "swap" else ins[i],
                dst_ref=outs[i].at[me],
                send_sem=send_sem.at[i, k],
                recv_sem=recv_sem.at[i, k],
                device_id=peer(to),
                device_id_type=MESH,
            )
            copy.start()
            sends.append((copy, i, k))
    for copy, i, k in sends:
        copy.wait_send()
    for copy, i, k in sends:
        origin = lax.rem(me + size - k, size)
        pltpu.make_async_remote_copy(
            src_ref=outs[i].at[origin],
            dst_ref=outs[i].at[origin],
            send_sem=send_sem.at[i, k],
            recv_sem=recv_sem.at[i, k],
            device_id=peer(origin),
            device_id_type=MESH,
        ).wait_recv()
    for own in owns:
        own.wait()


def greet(groups):
    barrier = pltpu.get_barrier_semaphore()
    for me, size, peer in groups:
        for k in range(1, size):
            pl.semaphore_signal(
                barrier, inc=1, device_id=peer(lax.rem(me + k, size)), device_id_type=MESH
            )
    return barrier, sum(size - 1 for _, size, _ in groups)


def remote(src, dst, send_sem, recv_sem, device):
    return pltpu.make_async_remote_copy(
        src_ref=src,
        dst_ref=dst,
        send_sem=send_sem,
        recv_sem=recv_sem,
        device_id=device,
        device_id_type=MESH,
    )


def turn_kernel(
    block_ref, mask_ref, data_ref, masks_ref,
    t_send, t_recv, m_send, m_recv, x_send, x_recv, own_sem,
):
    me, size, peer = place("tm")
    x, wide, beside = place("x")
    barrier, count = greet([(me, size, peer), (x, wide, beside)])
    own = pltpu.make_async_copy(block_ref.at[me], data_ref.at[x, me], own_sem.at[0])
    own_mask = pltpu.make_async_copy(mask_ref, masks_ref.at[me], own_sem.at[1])
    own.start()
    own_mask.start()
    pl.semaphore_wait(barrier, count)
    order = sorted(range(1, size), key=lambda k: min(k, size - k))
    pending = []

    def step_x(k, j, src, owner, group, by):
        copy = remote(
            src,
            data_ref.at[owner, group],
            x_send.at[k, j],
            x_recv.at[k, j],
            beside(lax.rem(x + by, wide)),
        )
        copy.start()
        pending.append(copy)

    def forward(k, src, group):
        step_x(k, 1, src, x, group, 1)
        step_x(k, 3, src, x, group, wide - 1)

    def land_x(k, j, group):
        origin = lax.rem(x + wide - j, wide)
        landed = data_ref.at[origin, group]
        remote(landed, landed, x_send.at[k, j], x_recv.at[k, j], beside(origin)).wait_recv()
        return origin, landed

    def relay(n):
        k = ([0] + order)[n]
        group = lax.rem(me + size - k, size)
        for j in (1, 3):
            origin, landed = land_x(k, j, group)
            if (j == 1) == (n % 4 in (0, 3)):
                step_x(k, 2, landed, origin, group, j)

    for k in order:
        to = lax.rem(me + k, size)
        copy = remote(
            block_ref.at[to], data_ref.at[x, me], t_send.at[k], t_recv.at[k], peer(to)
        )
        copy.start()
        pending.append(copy)
    forward(0, block_ref.at[me], me)
    for k in order:
        to = lax.rem(me + k, size)
        copy = remote(mask_ref, masks_ref.at[me], m_send.at[k], m_recv.at[k], peer(to))
        copy.start()
        pending.append(copy)
    for n, k in enumerate(order):
        origin = lax.rem(me + size - k, size)
        landed = data_ref.at[x, origin]
        remote(landed, landed, t_send.at[k], t_recv.at[k], peer(origin)).wait_recv()
        forward(k, landed, origin)
        if n >= 3:
            relay(n - 3)
    for k in order:
        origin = lax.rem(me + size - k, size)
        landed = masks_ref.at[origin]
        remote(landed, landed, m_send.at[k], m_recv.at[k], peer(origin)).wait_recv()
    for n in range(size - 4, size):
        relay(n)
    for k in [0] + order:
        land_x(k, 2, lax.rem(me + size - k, size))
    for copy in pending:
        copy.wait_send()
    own.wait()
    own_mask.wait()


def turn(blocks, mask):
    size = 2 * NY
    vmem = pl.BlockSpec(memory_space=pltpu.VMEM)
    dma = pltpu.SemaphoreType.DMA
    return pl.pallas_call(
        turn_kernel,
        out_shape=[
            jax.ShapeDtypeStruct((NX,) + blocks.shape, blocks.dtype),
            jax.ShapeDtypeStruct((size,) + mask.shape, mask.dtype),
        ],
        in_specs=[vmem] * 2,
        out_specs=[vmem] * 2,
        scratch_shapes=[dma((size,))] * 4 + [dma((size, NX))] * 2 + [dma((2,))],
        compiler_params=pltpu.CompilerParams(collective_id=1, has_side_effects=True),
        name="turn",
    )(blocks, mask)


def exchange(axis, identity, *pairs):
    size = {"z": NZ, "x": NX, "tm": 2 * NY, "y": NY, "core": 2}[axis]
    modes = tuple(mode for mode, _ in pairs)
    arrays = [array for _, array in pairs]
    shapes = [
        jax.ShapeDtypeStruct(
            array.shape if mode == "swap" else (size,) + array.shape, array.dtype
        )
        for mode, array in pairs
    ]
    count = len(pairs)
    vmem = pl.BlockSpec(memory_space=pltpu.VMEM)
    return pl.pallas_call(
        functools.partial(exchange_kernel, axis, modes),
        out_shape=shapes,
        in_specs=[vmem] * count,
        out_specs=[vmem] * count,
        scratch_shapes=[
            pltpu.SemaphoreType.DMA((count, size)),
            pltpu.SemaphoreType.DMA((count, size)),
            pltpu.SemaphoreType.DMA((count,)),
        ],
        compiler_params=pltpu.CompilerParams(
            collective_id=identity, has_side_effects=True
        ),
        name=f"exchange_{axis}",
    )(*arrays)


def stack_one(index_ref, mask_ref, data_ref, result_ref, c):
    first = index_ref[c, 0:1, :]
    second = index_ref[c, 1:2, :]
    code = index_ref[c, 2:3, :]
    pairs = first.shape[1]
    block = data_ref.shape[2]

    def pick(rows):
        total = None
        for part in range(data_ref.shape[0]):
            lane = lax.broadcasted_iota(jnp.int32, (block, pairs), 0) + part * block
            chosen = jnp.where(lane == rows, 1.0, 0.0).astype(jnp.bfloat16)
            term = jnp.dot(data_ref[part], chosen, preferred_element_type=jnp.float32)
            total = term if total is None else total + term
        return total.reshape(total.shape[0] // 16, 2, 8, pairs)

    a = pick(first)
    b = pick(second)
    mask = mask_ref[:, pl.ds(c, 1), :]
    real = jnp.sum((a[:, 0] * b[:, 0] + a[:, 1] * b[:, 1]) * mask, axis=0)
    imag = jnp.sum((a[:, 0] * b[:, 1] - a[:, 1] * b[:, 0]) * mask, axis=0)
    value = jnp.concatenate([real, imag], axis=0)
    high = value.astype(jnp.bfloat16)
    low = (value - high.astype(jnp.float32)).astype(jnp.bfloat16)
    slots = result_ref.shape[2]
    slot = lax.broadcasted_iota(jnp.int32, (slots, pairs), 0)
    chosen = jnp.where(slot == code, 1.0, 0.0).astype(jnp.bfloat16)
    contract = (((1,), (1,)), ((), ()))
    result_ref[c] = lax.dot_general(
        high, chosen, contract, preferred_element_type=jnp.float32
    ) + lax.dot_general(low, chosen, contract, preferred_element_type=jnp.float32)


def stack_kernel(
    index_ref, mask_ref, data_ref, out_ref,
    result_ref, landed_ref, wide_ref, z_send, z_recv, y_send, y_recv, own_sem,
):
    z, deep, along = place("z")
    y, tall, above = place("y")
    width = out_ref.shape[3]
    barrier, count = greet([(z, deep, along), (y, tall, above)])

    def compute(k):
        stack_one(index_ref, wide_ref, data_ref, result_ref, lax.rem(z + k, deep))

    def send(k):
        to = lax.rem(z + k, deep)
        return remote(
            result_ref.at[to], landed_ref.at[z], z_send.at[k], z_recv.at[k], along(to)
        )

    def lanes(j):
        return pl.ds(pl.multiple_of(j * width, width), width)

    def share(k, origin, src_ref):
        own = pltpu.make_async_copy(
            src_ref.at[origin, :, lanes(y)], out_ref.at[y, origin], own_sem.at[k]
        )
        away = []
        for j in range(1, tall):
            to = lax.rem(y + j, tall)
            away.append(
                remote(
                    src_ref.at[origin, :, lanes(to)],
                    out_ref.at[y, origin],
                    y_send.at[k, j],
                    y_recv.at[k, j],
                    above(to),
                )
            )
        return own, away

    def forward(k, origin, src_ref):
        own, away = share(k, origin, src_ref)
        own.start()
        for copy in away:
            copy.start()

    def receive(k):
        origin = lax.rem(z + deep - k, deep)
        landed = landed_ref.at[origin]
        remote(landed, landed, z_send.at[k], z_recv.at[k], along(origin)).wait_recv()
        forward(k, origin, landed_ref)

    def offset(step):
        return lax.rem(3 * step + 4, deep)

    wide_ref[...] = mask_ref[...].astype(jnp.float32)
    compute(offset(0))
    pl.semaphore_wait(barrier, count)

    @pl.loop(1, deep)
    def _(step):
        compute(offset(step))

        @pl.when(step != 5)
        def _():
            send(offset(step - 1)).start()

        @pl.when(step == 4)
        def _():
            receive(7)

        @pl.when(step == 5)
        def _():
            forward(0, z, result_ref)

        @pl.when(step == 6)
        def _():
            receive(4)

        @pl.when(step == 7)
        def _():
            receive(2)

    send(1).start()
    for k in (5, 3, 6, 1):
        receive(k)
    for k in range(deep):
        if k:
            send(k).wait_send()
        origin = lax.rem(z + deep - k, deep)
        own, away = share(k, origin, landed_ref if k else result_ref)
        own.wait()
        for copy in away:
            copy.wait_send()
        for j in range(1, tall):
            below = lax.rem(y + tall - j, tall)
            arrived = out_ref.at[below, origin]
            remote(
                arrived, arrived, y_send.at[k, j], y_recv.at[k, j], above(below)
            ).wait_recv()


def stack_pairs(index, mask, data, slots):
    rows = 16
    vmem = pl.BlockSpec(memory_space=pltpu.VMEM)
    dma = pltpu.SemaphoreType.DMA
    return pl.pallas_call(
        stack_kernel,
        out_shape=jax.ShapeDtypeStruct((NY, NZ, rows, slots // NY), jnp.float32),
        in_specs=[vmem] * 3,
        out_specs=vmem,
        scratch_shapes=[pltpu.VMEM((NZ, rows, slots), jnp.float32)] * 2
        + [pltpu.VMEM(mask.shape, jnp.float32)]
        + [dma((NZ,))] * 2
        + [dma((NZ, NY))] * 2
        + [dma((NZ,))],
        compiler_params=pltpu.CompilerParams(collective_id=2, has_side_effects=True),
        name="stack_pairs",
    )(index, mask, data)


def lag_kernel(
    stacked_ref, cos_c_ref, sin_c_ref, cos_f_ref, sin_f_ref, out_ref,
    part_ref, landed_ref, send_sem, recv_sem,
):
    core, size, peer = place("core")
    barrier, count = greet([(core, size, peer)])
    stacked = stacked_ref[...]
    high = stacked.astype(jnp.bfloat16)
    low = (stacked - high.astype(jnp.float32)).astype(jnp.bfloat16)
    chunks, rows, width = landed_ref.shape
    other = 1 - core

    def product(left, right):
        return lax.dot_general(
            left, right, (((0,), (0,)), ((), ())), preferred_element_type=jnp.float32
        )

    def copy(n):
        return remote(
            part_ref.at[n, pl.ds(pl.multiple_of(other * rows, rows), rows)],
            landed_ref.at[n],
            send_sem.at[n],
            recv_sem.at[n],
            peer(other),
        )

    for n in range(chunks):
        lags = pl.ds(n * width, width)
        cos_c, sin_c = cos_c_ref[:, lags][None, :, None], sin_c_ref[:, lags][None, :, None]
        cos_f, sin_f = cos_f_ref[:, :, lags][:, None], sin_f_ref[:, :, lags][:, None]
        real = cos_c * cos_f - sin_c * sin_f
        imag = -(sin_c * cos_f + cos_c * sin_f)
        table = jnp.stack([real, imag], axis=2).reshape(stacked.shape[0], width)
        table_high = table.astype(jnp.bfloat16)
        table_low = (table - table_high.astype(jnp.float32)).astype(jnp.bfloat16)
        part_ref[n] = (
            product(high, table_high)
            + product(high, table_low)
            + product(low, table_high)
        )
        if n == 0:
            pl.semaphore_wait(barrier, count)
        else:
            copy(n - 1).start()
    copy(chunks - 1).start()
    for n in range(chunks):
        copy(n).wait_recv()
        own = part_ref[n, pl.ds(pl.multiple_of(core * rows, rows), rows)]
        out_ref[:, pl.ds(n * width, width)] = own + landed_ref[n]
    for n in range(chunks):
        copy(n).wait_send()


def lag_product(stacked, angles_of, chunks=4):
    rows = stacked.shape[1] // 2
    width = LAGS // chunks
    vmem = pl.BlockSpec(memory_space=pltpu.VMEM)
    dma = pltpu.SemaphoreType.DMA
    return pl.pallas_call(
        lag_kernel,
        out_shape=jax.ShapeDtypeStruct((rows, LAGS), jnp.float32),
        in_specs=[vmem] * 5,
        out_specs=vmem,
        scratch_shapes=[
            pltpu.VMEM((chunks, 2 * rows, width), jnp.float32),
            pltpu.VMEM((chunks, rows, width), jnp.float32),
            dma((chunks,)),
            dma((chunks,)),
        ],
        compiler_params=pltpu.CompilerParams(collective_id=3, has_side_effects=True),
        name="lag_product",
    )(stacked, *angles_of)


def angles(bins, scale_bins):
    lag = jnp.arange(LAGS, dtype=jnp.int32)[None, :] - LAGS // 2
    phase = (bins[:, None] * lag) % (2 * scale_bins)
    phase = phase.astype(jnp.float32) * (jnp.pi / scale_bins)
    return jnp.cos(phase), jnp.sin(phase)


def half_angles(bins):
    core = lax.axis_index("tm") % 2
    coarse = jnp.arange(NZ, dtype=jnp.int32) * (bins // NZ)
    number = jnp.arange(NY * 8, dtype=jnp.int32)
    fine = (number // 8 * 2 + core) * 8 + number % 8
    cos_c, sin_c = angles(coarse, bins)
    cos_f, sin_f = angles(fine, bins)
    scale = 1.0 / bins**0.5
    return (
        cos_c * scale,
        sin_c * scale,
        cos_f.reshape(NY, 8, LAGS),
        sin_f.reshape(NY, 8, LAGS),
    )


def local(spectra, pair_list, pair_stations, owner_code):
    stations, width = spectra.shape[1:]
    bins = width // 2
    catalogue = owner_code.shape[0]
    groups = 2 * NY
    slots = 2 * catalogue
    f = bins // (NZ * groups)
    angles_of = half_angles(bins)
    shard, inner = pair_stations // stations, pair_stations % stations
    column = (shard % NX) * (NZ * stations) + (shard // NX) * stations + inner
    number = jnp.arange(catalogue, dtype=jnp.int32)
    listed = jnp.any(number[:, None] == pair_list[0, 0][None, :], axis=1)
    index = jnp.concatenate(
        [
            column,
            owner_code[None],
            listed.astype(jnp.int32)[None],
        ]
    )
    blocks = spectra[0].reshape(stations, 2, NZ, bins // NZ).transpose(2, 0, 1, 3)
    blocks = blocks.reshape(NZ, stations, 2 * bins // NZ)
    blocks, index = exchange("z", 0, ("swap", blocks), ("copy", index))
    mask = index[:, 3, :].astype(jnp.bfloat16)
    turned = blocks.reshape(NZ * stations, 2, groups, f).transpose(2, 1, 3, 0)
    data, mask = turn(turned.reshape(groups, 2 * f, NZ * stations), mask)
    data = data.reshape(NX, groups * 2 * f, NZ * stations)
    stacked = stack_pairs(index, mask, data, slots)
    return lag_product(stacked.reshape(bins, slots // NY), angles_of)


def solution(mesh):
    return jax.shard_map(
        local,
        mesh=mesh,
        in_specs=(P("tm", "sta", None), P("tm", "sta", None), P(None, "sta"), P("sta")),
        out_specs=P(("tm", "sta"), None),
        check_vma=False,
    )
```
